128 devices in a mesh: row: 8 (over y, core), col: 16 (over z, x).
Axes of the slice: x: 4, y: 4, z: 4, core: 2. Of those that a mesh axis runs over, the one named last changes fastest.
Arguments:
- pair_rows: int32 [18432, 768], P(('row', 'col')), may hold values from 0 to 4095, as said below
- pair_cols: int32 [18432, 768], P(('row', 'col')), may hold values from 0 to 8191
- pair_weights: float32 [18432, 768], P(('row', 'col')), may hold values from 0.2 to 6, as said below
- block_counts: int32 [18432], P(('row', 'col')), may hold values from 576 to 768, as said below
Outputs:
- balanced: float32 [4096, 8192], P('row', 'col')
- row_bias: float32 [4096], P('row')
- col_bias: float32 [8192], P('col')
The draws below stay inside these ranges and needn't reach their ends.
Inputs may be any that keep to these rules, and one draw needn't show every extreme that they name: `pair_rows`: all entries of one block lie in one aligned 128 x 128 square of one 512 x 512 tile of the map (tiles counted from bin 0 along both sides). Among the blocks of one device, every tile whose tile row differs from its tile column has exactly one block, and every tile whose tile row equals its tile column has exactly 3. `pair_weights`: positive weights. Only the first block_counts entries of a block are read pairs.
All inputs are finite; a program needn't handle non-finite values.
Results may differ from the reference program's by a relative error of at most 0.0001.
Values sent between devices are 32-bit elements; how exact they have to be, the bound alone decides.
No kernel may reach another device: no remote copies, remote signals or barrier semaphores. Data moves between devices by JAX's collectives and lax.ppermute only.
A program may use at most 64 MiB of HBM per device.

```python
import jax
import jax.numpy as jnp
from jax import lax

TILE = 512
SUB = 128
SLOT = 3
CAP = 768
SWEEPS = 2
R_BINS = 4096
C_BINS = 8192
BLK_DEV = 144
NBLK = 18432
N_ROW = 8
N_COL = 16
DEVICES = 128


def shuffle_order(order_seed):
    return jax.random.permutation(order_seed, BLK_DEV)


def block_plan(key):
    order_key, square_key = jax.random.split(key)
    off_count = DEVICES - N_ROW
    tile_all = jnp.arange(DEVICES, dtype=jnp.int32)
    on_diagonal = (tile_all // N_COL == tile_all % N_COL).astype(jnp.int32)
    off_tiles = jnp.argsort(on_diagonal, stable=True)[:off_count].astype(jnp.int32)
    source_keys = jax.random.split(order_key, DEVICES)
    logical = jax.vmap(shuffle_order)(source_keys).reshape(-1).astype(jnp.int32)
    diag_row = (logical - off_count) // SLOT
    tile_ids = jnp.where(logical < off_count, off_tiles[jnp.minimum(logical, off_count - 1)], diag_row * N_COL + diag_row)
    per_side = TILE // SUB
    square_ids = jax.random.randint(square_key, (NBLK,), 0, per_side * per_side)
    return (tile_ids.astype(jnp.int32), square_ids.astype(jnp.int32))


def draw_pair_rows(key, part):
    tile_ids, square_ids = block_plan(jax.random.fold_in(key, 101))
    per_side = TILE // SUB
    offset = jax.random.randint(jax.random.fold_in(key, 202), (NBLK, CAP), 0, SUB)
    corner = tile_ids // N_COL * TILE + square_ids // per_side * SUB
    return (corner[:, None] + offset).astype(jnp.int32)


def draw_pair_cols(key, part):
    tile_ids, square_ids = block_plan(jax.random.fold_in(key, 101))
    per_side = TILE // SUB
    offset = jax.random.randint(jax.random.fold_in(key, 303), (NBLK, CAP), 0, SUB)
    corner = tile_ids % N_COL * TILE + square_ids % per_side * SUB
    return (corner[:, None] + offset).astype(jnp.int32)


def draw_pair_weights(key, part):
    tile_ids, square_ids = block_plan(jax.random.fold_in(key, 101))
    rise = (tile_ids // N_COL).astype(jnp.float32) / (N_ROW - 1.0)
    base = jax.random.uniform(jax.random.fold_in(key, 505), (NBLK, CAP), jnp.float32, 0.2, 1.0)
    scale = 1.0 + 2.0 * rise
    return (base * scale[:, None]).astype(jnp.float32)


def draw_block_counts(key, part):
    counts = jax.random.randint(jax.random.fold_in(key, 404), (NBLK,), 3 * CAP // 4, CAP + 1)
    first_block = jnp.arange(NBLK, dtype=jnp.int32) % BLK_DEV == 0
    return jnp.where(first_block, CAP, counts).astype(jnp.int32)


def setup_inputs(seed: int = 0) -> dict:
    streams_of = jax.random.split(jax.random.key(seed), 5)
    return {
        "pair_rows": draw_pair_rows(jax.random.fold_in(streams_of[4], 71), 0),
        "pair_cols": draw_pair_cols(jax.random.fold_in(streams_of[4], 71), 0),
        "pair_weights": draw_pair_weights(jax.random.fold_in(streams_of[4], 71), 0),
        "block_counts": draw_block_counts(jax.random.fold_in(streams_of[4], 71), 0),
    }


def reference(pair_rows, pair_cols, pair_weights, block_counts):
    entry_pos = lax.broadcasted_iota(jnp.int32, (NBLK, CAP), 1)
    valid = entry_pos < block_counts[:, None]
    weights = jnp.where(valid, pair_weights, 0.0).astype(jnp.float32)
    contact = jnp.zeros((R_BINS, C_BINS), jnp.float32)
    contact = contact.at[pair_rows.reshape(-1).astype(jnp.int32), pair_cols.reshape(-1).astype(jnp.int32)].add(weights.reshape(-1))
    balanced = contact + 0.015625
    row_bias = jnp.ones((R_BINS,), jnp.float32)
    col_bias = jnp.ones((C_BINS,), jnp.float32)
    for sweep_idx in range(SWEEPS):
        row_sums = jnp.sum(balanced, axis=1)
        row_mean = jnp.sum(row_sums) / R_BINS
        ratio = row_sums / row_mean
        balanced = balanced / ratio[:, None]
        row_bias = row_bias * ratio
        col_sums = jnp.sum(balanced, axis=0)
        col_mean = jnp.sum(col_sums) / C_BINS
        factor = col_sums / col_mean
        balanced = balanced / factor[None, :]
        col_bias = col_bias * factor
    return balanced, row_bias, col_bias
```

```python
import jax
import jax.numpy as jnp
from jax import lax
from jax.experimental import pallas as pl
from jax.experimental.pallas import tpu as pltpu
from jax.sharding import PartitionSpec as P

TILE = 512
SUB = 128
LANES = 128
SIDE = TILE // SUB
SWEEPS = 2

prior_count = 0.015625


def pack_kernel(tile_ref, counts_ref, rows_ref, cols_ref, wgt_ref, send_ref, seen_ref):
    blocks, cap = rows_ref.shape
    chunks = cap // LANES
    n_col = 16
    for i in range(seen_ref.shape[0]):
        seen_ref[i] = 0

    @pl.loop(0, blocks // 8)
    def _(group):
        at = pl.ds(pl.multiple_of(group * 8, 8), 8)
        place = (rows_ref[at, :] & (TILE - 1)) * TILE + (cols_ref[at, :] & (TILE - 1))
        place = place.astype(jnp.float32)
        wgt = wgt_ref[at, :]
        entry = lax.broadcasted_iota(jnp.int32, (1, cap), 1)
        for r in range(8):
            b = group * 8 + r
            tile = tile_ref[b]
            tile_row = tile // n_col
            tile_col = tile % n_col
            diagonal = tile_row == tile_col
            rank = jnp.where(diagonal, seen_ref[tile_row], 0)
            seen_ref[tile_row] = seen_ref[tile_row] + jnp.where(diagonal, 1, 0)
            dest = jnp.where(rank == 2, (tile_row ^ 1) * n_col + tile_col, tile)
            slot = jnp.minimum(rank, 1)
            kept = jnp.where(entry < counts_ref[b], wgt[r : r + 1, :], 0.0)
            parts = [place[r : r + 1, LANES * k : LANES * (k + 1)] for k in range(chunks)]
            parts += [kept[:, LANES * k : LANES * (k + 1)] for k in range(chunks)]
            base = slot * 2 * chunks
            for k, part in enumerate(parts):
                send_ref[dest, pl.ds(base + k, 1), :] = part


def pack(tile, counts, rows, cols, wgt, devices):
    blocks, cap = rows.shape
    return pl.pallas_call(
        pack_kernel,
        out_shape=jax.ShapeDtypeStruct((devices, 4 * cap // LANES, LANES), jnp.float32),
        in_specs=[pl.BlockSpec(memory_space=pltpu.SMEM)] * 2
        + [pl.BlockSpec(memory_space=pltpu.VMEM)] * 3,
        out_specs=pl.BlockSpec(memory_space=pltpu.VMEM),
        scratch_shapes=[pltpu.SMEM((8,), jnp.int32)],
        name="pack",
    )(tile, counts, rows, cols, wgt)


def square_of(x, chunks):
    place = x[:chunks].astype(jnp.int32)
    wgt = x[chunks:]
    local_row = ((place >> 9) & (SUB - 1)).astype(jnp.float32)
    local_col = (place & (SUB - 1)).astype(jnp.float32)
    high = wgt.astype(jnp.bfloat16).astype(jnp.float32)
    rest = wgt - high
    bins = lax.broadcasted_iota(jnp.int32, (SUB, LANES), 0).astype(jnp.bfloat16)
    one = jnp.ones((SUB, LANES), jnp.bfloat16)
    zero = jnp.zeros((SUB, LANES), jnp.bfloat16)

    def spread(v, k):
        return jnp.broadcast_to(v[k : k + 1], (SUB, LANES)).astype(jnp.bfloat16)

    row_hot, high_hot, rest_hot = [], [], []
    for k in range(chunks):
        row_hot.append(jnp.where(spread(local_row, k) == bins, one, zero))
        hit = spread(local_col, k) == bins
        high_hot.append(jnp.where(hit, spread(high, k), zero))
        rest_hot.append(jnp.where(hit, spread(rest, k), zero))
    row_hot = jnp.concatenate(row_hot, axis=1)
    col_hot = jnp.concatenate(
        [jnp.concatenate(high_hot, axis=1), jnp.concatenate(rest_hot, axis=1)], axis=0
    )
    both = lax.dot_general(
        row_hot, col_hot, (((1,), (1,)), ((), ())), preferred_element_type=jnp.float32
    )
    return both[:, :SUB] + both[:, SUB:]


def add_blocks(got_ref, slot, acc_ref, unroll):
    sources = got_ref.shape[0]
    chunks = got_ref.shape[1] // 4

    @pl.loop(0, sources // unroll)
    def _(step):
        for u in range(unroll):
            x = got_ref[step * unroll + u, 2 * chunks * slot : 2 * chunks * (slot + 1), :]
            head = x[0, 0].astype(jnp.int32)
            square = (head >> 16) * SIDE + ((head >> 7) & (SIDE - 1))
            acc_ref[square] += square_of(x, chunks)


def write_tile(acc_ref, out_ref):
    for i in range(SIDE):
        for j in range(SIDE):
            out_ref[SUB * i : SUB * (i + 1), SUB * j : SUB * (j + 1)] = acc_ref[i * SIDE + j]


def extra_kernel(got_ref, out_ref, acc_ref):
    me_row = lax.axis_index("row")
    me_col = lax.axis_index("col")
    step = pl.program_id(0)

    @pl.when((me_row // 2) == (me_col // 2))
    def _():
        @pl.when(step == 0)
        def _():
            acc_ref[...] = jnp.zeros_like(acc_ref)

        add_blocks(got_ref, 1, acc_ref, 4)

        @pl.when(step == pl.num_programs(0) - 1)
        def _():
            write_tile(acc_ref, out_ref)


def main_kernel(got_ref, extra_ref, out_ref, acc_ref):
    me_row = lax.axis_index("row")
    me_col = lax.axis_index("col")
    step = pl.program_id(0)

    @pl.when(step == 0)
    def _():
        acc_ref[...] = jnp.zeros_like(acc_ref)

    add_blocks(got_ref, 0, acc_ref, 4)

    @pl.when(step == pl.num_programs(0) - 1)
    def _():
        write_tile(acc_ref, out_ref)

        @pl.when(me_row == me_col)
        def _():
            out_ref[...] += extra_ref[...]


bin_steps = 8


def bin_extra(got):
    sources = got.shape[0]
    return pl.pallas_call(
        extra_kernel,
        grid=(bin_steps,),
        out_shape=jax.ShapeDtypeStruct((TILE, TILE), jnp.float32),
        in_specs=[pl.BlockSpec((sources // bin_steps,) + got.shape[1:], lambda i: (i, 0, 0))],
        out_specs=pl.BlockSpec((TILE, TILE), lambda i: (0, 0)),
        scratch_shapes=[pltpu.VMEM((SIDE * SIDE, SUB, SUB), jnp.float32)],
        name="bin_extra",
    )(got)


def bin_main(got, extra):
    sources = got.shape[0]
    return pl.pallas_call(
        main_kernel,
        grid=(bin_steps,),
        out_shape=jax.ShapeDtypeStruct((TILE, TILE), jnp.float32),
        in_specs=[
            pl.BlockSpec((sources // bin_steps,) + got.shape[1:], lambda i: (i, 0, 0)),
            pl.BlockSpec((TILE, TILE), lambda i: (0, 0)),
        ],
        out_specs=pl.BlockSpec((TILE, TILE), lambda i: (0, 0)),
        scratch_shapes=[pltpu.VMEM((SIDE * SIDE, SUB, SUB), jnp.float32)],
        name="bin_main",
    )(got, extra)


def to_lanes(column):
    return jnp.concatenate(
        [
            jnp.sum(jnp.where(same_lane(), column[LANES * k : LANES * (k + 1)], 0.0), axis=0, keepdims=True)
            for k in range(TILE // LANES)
        ],
        axis=0,
    )


def same_lane():
    down = lax.broadcasted_iota(jnp.int32, (LANES, LANES), 0)
    across = lax.broadcasted_iota(jnp.int32, (LANES, LANES), 1)
    return down == across


def to_column(vec):
    return jnp.concatenate(
        [
            jnp.sum(jnp.where(same_lane(), vec[k : k + 1], 0.0), axis=1, keepdims=True)
            for k in range(vec.shape[0])
        ],
        axis=0,
    )


def as_row(vec):
    return jnp.concatenate([vec[k : k + 1] for k in range(vec.shape[0])], axis=1)


def from_row(row):
    return jnp.concatenate(
        [row[:, LANES * k : LANES * (k + 1)] for k in range(TILE // LANES)], axis=0
    )


def first_kernel(part_ref, moved_ref, tile_ref, rows_ref):
    tile = part_ref[...] + moved_ref[...] + prior_count
    tile_ref[...] = tile
    sums = to_lanes(jnp.sum(tile, axis=1, keepdims=True))
    for d in range(rows_ref.shape[0]):
        rows_ref[d] = sums


def down_first_kernel(tile_ref, got_ref, out_ref):
    row_sums = jnp.sum(got_ref[...], axis=0)
    total = jnp.sum(row_sums, axis=1, keepdims=True)
    sums = from_row(jnp.sum(tile_ref[...] / to_column(row_sums), axis=0, keepdims=True))
    send = jnp.concatenate([sums, jnp.broadcast_to(total, sums.shape)], axis=0)
    for d in range(out_ref.shape[0]):
        out_ref[d] = send


def across_kernel(tile_ref, got_ref, out_ref):
    vec = jnp.sum(got_ref[:, : TILE // LANES, :], axis=0) * 2.0
    sums = to_lanes(jnp.sum(tile_ref[...] / as_row(vec), axis=1, keepdims=True))
    for d in range(out_ref.shape[0]):
        out_ref[d] = sums


def down_kernel(tile_ref, got_ref, out_ref):
    vec = jnp.sum(got_ref[...], axis=0)
    sums = from_row(jnp.sum(tile_ref[...] / to_column(vec), axis=0, keepdims=True))
    for d in range(out_ref.shape[0]):
        out_ref[d] = sums


def last_kernel(r_bins, tile_ref, first_ref, across_ref, down_ref, out_ref, row_ref, col_ref):
    total = jnp.sum(first_ref[:, TILE // LANES :, 0:1], axis=(0, 1), keepdims=True)[0]
    row_mean = total / r_bins
    row_bias = jnp.sum(across_ref[...], axis=0) / row_mean
    col_bias = jnp.sum(down_ref[...], axis=0) * 2.0
    row_ref[...] = row_bias
    col_ref[...] = col_bias
    out_ref[...] = tile_ref[...] / (to_column(row_bias) * as_row(col_bias))


def on_device(pair_rows, pair_cols, pair_weights, block_counts):
    n_row = lax.axis_size("row")
    n_col = lax.axis_size("col")
    devices = n_row * n_col
    r_bins = float(TILE * n_row)
    lines = TILE // LANES
    tile_id = (pair_rows[:, 0] >> 9) * n_col + (pair_cols[:, 0] >> 9)
    send = pack(tile_id, block_counts, pair_rows, pair_cols, pair_weights, devices)
    got = lax.all_to_all(send, ("row", "col"), split_axis=0, concat_axis=0, tiled=True)
    extra = bin_extra(got)
    handed = [((r ^ 1) * n_col + r, r * n_col + r) for r in range(n_row)]
    moved = lax.ppermute(extra, ("row", "col"), handed)
    part = bin_main(got, extra)
    tile_type = jax.ShapeDtypeStruct((TILE, TILE), jnp.float32)
    vec_type = jax.ShapeDtypeStruct((lines, LANES), jnp.float32)

    def sent(n, k=lines):
        return jax.ShapeDtypeStruct((n, k, LANES), jnp.float32)

    def swap(x, axis):
        return lax.all_to_all(x, axis, split_axis=0, concat_axis=0, tiled=True)

    tile, rows_part = pl.pallas_call(first_kernel, out_shape=(tile_type, sent(n_col)), name="first")(part, moved)
    rows_got = swap(rows_part, "col")
    first_part = pl.pallas_call(down_first_kernel, out_shape=sent(n_row, 2 * lines), name="down_first")(tile, rows_got)
    first_got = swap(first_part, "row")
    across_part = pl.pallas_call(across_kernel, out_shape=sent(n_col), name="across")(tile, first_got)
    across_got = swap(across_part, "col")
    down_part = pl.pallas_call(down_kernel, out_shape=sent(n_row), name="down")(tile, across_got)
    down_got = swap(down_part, "row")
    balanced, row_bias, col_bias = pl.pallas_call(
        lambda *refs: last_kernel(r_bins, *refs), out_shape=(tile_type, vec_type, vec_type), name="last"
    )(tile, first_got, across_got, down_got)
    return (balanced, row_bias.reshape(-1), col_bias.reshape(-1))


def solution(mesh):
    return jax.shard_map(
        on_device,
        mesh=mesh,
        in_specs=(
            P(("row", "col"), None),
            P(("row", "col"), None),
            P(("row", "col"), None),
            P(("row", "col")),
        ),
        out_specs=(P("row", "col"), P("row"), P("col")),
        check_vma=False,
    )
```

```python
import jax
import jax.numpy as jnp
from jax import lax
from jax.experimental import pallas as pl
from jax.experimental.pallas import tpu as pltpu
from jax.sharding import PartitionSpec as P

TILE = 512
SUB = 128
LANES = 128
SIDE = TILE // SUB
SWEEPS = 2

prior_count = 0.015625


def pack_kernel(counts_ref, rows_ref, cols_ref, wgt_ref, send_ref, kept_ref, seen_ref):
    blocks, cap = rows_ref.shape
    chunks = cap // LANES
    n_col = 16
    for i in range(seen_ref.shape[0]):
        seen_ref[i] = 0

    @pl.loop(0, blocks // 8)
    def _(group):
        at = pl.ds(pl.multiple_of(group * 8, 8), 8)
        rows = rows_ref[at, :]
        cols = cols_ref[at, :]
        place = ((rows & (TILE - 1)) * TILE + (cols & (TILE - 1))).astype(jnp.float32)
        tiles = (rows[:, :1] // TILE) * n_col + cols[:, :1] // TILE
        entry = lax.broadcasted_iota(jnp.int32, (8, cap), 1)
        line = lax.broadcasted_iota(jnp.int32, (8, cap), 0)
        count = jnp.zeros((8, cap), jnp.int32)
        for r in range(8):
            count = jnp.where(line == r, counts_ref[group * 8 + r], count)
        kept = jnp.where(entry < count, wgt_ref[at, :], 0.0)
        kept_ref[at, :] = kept
        for r in range(8):
            tile = tiles[r, 0]
            tile_row = tile // n_col
            tile_col = tile % n_col
            diagonal = tile_row == tile_col
            rank = jnp.where(diagonal, seen_ref[tile_row], 0)
            seen_ref[tile_row] = seen_ref[tile_row] + jnp.where(diagonal, 1, 0)
            dest = jnp.where(rank == 2, (tile_row ^ 1) * n_col + tile_col, tile)
            slot = jnp.minimum(rank, 1)
            parts = [
                x[r : r + 1, LANES * k : LANES * (k + 1)] for x in (place, kept) for k in range(chunks)
            ]
            base = slot * 2 * chunks
            for k, part in enumerate(parts):
                send_ref[dest, pl.ds(base + k, 1), :] = part


def pack(counts, rows, cols, wgt, devices):
    blocks, cap = rows.shape
    return pl.pallas_call(
        pack_kernel,
        out_shape=(
            jax.ShapeDtypeStruct((devices, 4 * cap // LANES, LANES), jnp.float32),
            jax.ShapeDtypeStruct(wgt.shape, jnp.float32),
        ),
        in_specs=[pl.BlockSpec(memory_space=pltpu.SMEM)] + [pl.BlockSpec(memory_space=pltpu.VMEM)] * 3,
        out_specs=(pl.BlockSpec(memory_space=pltpu.VMEM),) * 2,
        scratch_shapes=[pltpu.SMEM((8,), jnp.int32)],
        name="pack",
    )(counts, rows, cols, wgt)


def row_share_kernel(n_col, rows_ref, kept_ref, out_ref, acc_ref):
    blocks, cap = rows_ref.shape
    acc_ref[...] = jnp.zeros_like(acc_ref)
    bins = lax.broadcasted_iota(jnp.int32, (SUB, LANES), 0)

    @pl.loop(0, blocks // 8)
    def _(group):
        at = pl.ds(pl.multiple_of(group * 8, 8), 8)
        rows = rows_ref[at, :]
        kept = kept_ref[at, :]
        local = rows & (SUB - 1)
        strips = rows[:, :1] // SUB
        for r in range(8):
            total = jnp.zeros((SUB, LANES), jnp.float32)
            for k in range(cap // LANES):
                lanes = slice(LANES * k, LANES * (k + 1))
                total += jnp.where(local[r : r + 1, lanes] == bins, kept[r : r + 1, lanes], 0.0)
            acc_ref[strips[r, 0]] += total

    for strip in range(acc_ref.shape[0]):
        column = jnp.sum(acc_ref[strip], axis=1, keepdims=True)
        sums = jnp.sum(jnp.where(same_lane(), column, 0.0), axis=0, keepdims=True)
        row, line = divmod(strip, TILE // SUB)
        for c in range(n_col):
            out_ref[row * n_col + c, line : line + 1, :] = sums


def row_share(rows, kept, n_row, n_col):
    return pl.pallas_call(
        lambda *refs: row_share_kernel(n_col, *refs),
        out_shape=jax.ShapeDtypeStruct((n_row * n_col, TILE // LANES, LANES), jnp.float32),
        scratch_shapes=[pltpu.VMEM((n_row * TILE // SUB, SUB, LANES), jnp.float32)],
        cost_estimate=pl.CostEstimate(flops=10**9, bytes_accessed=10**6, transcendentals=0),
        name="row_share",
    )(rows, kept)


def square_of(x, chunks):
    place = x[:chunks].astype(jnp.int32)
    wgt = x[chunks:]
    local_row = ((place >> 9) & (SUB - 1)).astype(jnp.float32)
    local_col = (place & (SUB - 1)).astype(jnp.float32)
    high = wgt.astype(jnp.bfloat16).astype(jnp.float32)
    rest = wgt - high
    bins = lax.broadcasted_iota(jnp.int32, (SUB, LANES), 0).astype(jnp.bfloat16)
    one = jnp.ones((SUB, LANES), jnp.bfloat16)
    zero = jnp.zeros((SUB, LANES), jnp.bfloat16)

    def spread(v, k):
        return jnp.broadcast_to(v[k : k + 1], (SUB, LANES)).astype(jnp.bfloat16)

    row_hot, high_hot, rest_hot = [], [], []
    for k in range(chunks):
        row_hot.append(jnp.where(spread(local_row, k) == bins, one, zero))
        hit = spread(local_col, k) == bins
        high_hot.append(jnp.where(hit, spread(high, k), zero))
        rest_hot.append(jnp.where(hit, spread(rest, k), zero))
    row_hot = jnp.concatenate(row_hot, axis=1)
    col_hot = jnp.concatenate(
        [jnp.concatenate(high_hot, axis=1), jnp.concatenate(rest_hot, axis=1)], axis=0
    )
    both = lax.dot_general(
        row_hot, col_hot, (((1,), (1,)), ((), ())), preferred_element_type=jnp.float32
    )
    return both[:, :SUB] + both[:, SUB:]


def add_blocks(got_ref, slot, acc_ref, unroll):
    sources = got_ref.shape[0]
    chunks = got_ref.shape[1] // 4

    @pl.loop(0, sources // unroll)
    def _(step):
        for u in range(unroll):
            x = got_ref[step * unroll + u, 2 * chunks * slot : 2 * chunks * (slot + 1), :]
            head = x[0, 0].astype(jnp.int32)
            square = (head >> 16) * SIDE + ((head >> 7) & (SIDE - 1))
            acc_ref[square] += square_of(x, chunks)


def write_tile(acc_ref, out_ref):
    for i in range(SIDE):
        for j in range(SIDE):
            out_ref[SUB * i : SUB * (i + 1), SUB * j : SUB * (j + 1)] = acc_ref[i * SIDE + j]


def extra_kernel(got_ref, out_ref, acc_ref):
    me_row = lax.axis_index("row")
    me_col = lax.axis_index("col")
    step = pl.program_id(0)

    @pl.when((me_row // 2) == (me_col // 2))
    def _():
        @pl.when(step == 0)
        def _():
            acc_ref[...] = jnp.zeros_like(acc_ref)

        add_blocks(got_ref, 1, acc_ref, bin_unroll)

        @pl.when(step == pl.num_programs(0) - 1)
        def _():
            write_tile(acc_ref, out_ref)


def main_kernel(got_ref, extra_ref, out_ref, acc_ref):
    me_row = lax.axis_index("row")
    me_col = lax.axis_index("col")
    step = pl.program_id(0)

    @pl.when(step == 0)
    def _():
        acc_ref[...] = jnp.zeros_like(acc_ref)

    add_blocks(got_ref, 0, acc_ref, bin_unroll)

    @pl.when(step == pl.num_programs(0) - 1)
    def _():
        write_tile(acc_ref, out_ref)

        @pl.when(me_row == me_col)
        def _():
            out_ref[...] += extra_ref[...]


bin_steps = 4
bin_unroll = 8
bin_cost = pl.CostEstimate(flops=10**10, bytes_accessed=2 * 10**6, transcendentals=0)


def bin_extra(got):
    sources = got.shape[0]
    return pl.pallas_call(
        extra_kernel,
        grid=(bin_steps,),
        out_shape=jax.ShapeDtypeStruct((TILE, TILE), jnp.float32),
        in_specs=[pl.BlockSpec((sources // bin_steps,) + got.shape[1:], lambda i: (i, 0, 0))],
        out_specs=pl.BlockSpec((TILE, TILE), lambda i: (0, 0)),
        scratch_shapes=[pltpu.VMEM((SIDE * SIDE, SUB, SUB), jnp.float32)],
        cost_estimate=bin_cost,
        name="bin_extra",
    )(got)


def bin_main(got, extra):
    sources = got.shape[0]
    return pl.pallas_call(
        main_kernel,
        grid=(bin_steps,),
        out_shape=jax.ShapeDtypeStruct((TILE, TILE), jnp.float32),
        in_specs=[
            pl.BlockSpec((sources // bin_steps,) + got.shape[1:], lambda i: (i, 0, 0)),
            pl.BlockSpec((TILE, TILE), lambda i: (0, 0)),
        ],
        out_specs=pl.BlockSpec((TILE, TILE), lambda i: (0, 0)),
        scratch_shapes=[pltpu.VMEM((SIDE * SIDE, SUB, SUB), jnp.float32)],
        cost_estimate=bin_cost,
        name="bin_main",
    )(got, extra)


def to_lanes(column):
    return jnp.concatenate(
        [
            jnp.sum(jnp.where(same_lane(), column[LANES * k : LANES * (k + 1)], 0.0), axis=0, keepdims=True)
            for k in range(TILE // LANES)
        ],
        axis=0,
    )


def same_lane():
    down = lax.broadcasted_iota(jnp.int32, (LANES, LANES), 0)
    across = lax.broadcasted_iota(jnp.int32, (LANES, LANES), 1)
    return down == across


def to_column(vec):
    return jnp.concatenate(
        [
            jnp.sum(jnp.where(same_lane(), vec[k : k + 1], 0.0), axis=1, keepdims=True)
            for k in range(vec.shape[0])
        ],
        axis=0,
    )


def as_row(vec):
    return jnp.concatenate([vec[k : k + 1] for k in range(vec.shape[0])], axis=1)


def from_row(row):
    return jnp.concatenate(
        [row[:, LANES * k : LANES * (k + 1)] for k in range(TILE // LANES)], axis=0
    )


def first_kernel(c_bins, part_ref, moved_ref, got_ref, tile_ref, out_ref):
    tile = part_ref[...] + moved_ref[...] + prior_count
    tile_ref[...] = tile
    row_sums = jnp.sum(got_ref[...], axis=0) + c_bins * prior_count
    total = jnp.sum(row_sums, axis=1, keepdims=True)
    sums = from_row(jnp.sum(tile * to_column(1.0 / row_sums), axis=0, keepdims=True))
    send = jnp.concatenate([sums, jnp.broadcast_to(total, sums.shape)], axis=0)
    for d in range(out_ref.shape[0]):
        out_ref[d] = send


def across_kernel(wider, tile_ref, got_ref, out_ref):
    vec = jnp.sum(got_ref[:, : TILE // LANES, :], axis=0) * wider
    sums = to_lanes(jnp.sum(tile_ref[...] * as_row(1.0 / vec), axis=1, keepdims=True))
    for d in range(out_ref.shape[0]):
        out_ref[d] = sums


def down_kernel(tile_ref, got_ref, out_ref):
    vec = jnp.sum(got_ref[...], axis=0)
    sums = from_row(jnp.sum(tile_ref[...] * to_column(1.0 / vec), axis=0, keepdims=True))
    for d in range(out_ref.shape[0]):
        out_ref[d] = sums


def last_kernel(r_bins, wider, tile_ref, first_ref, across_ref, down_ref, out_ref, row_ref, col_ref):
    total = jnp.sum(first_ref[:, TILE // LANES :, 0:1], axis=(0, 1), keepdims=True)[0]
    row_mean = total / r_bins
    row_bias = jnp.sum(across_ref[...], axis=0) / row_mean
    col_bias = jnp.sum(down_ref[...], axis=0) * wider
    row_ref[...] = row_bias
    col_ref[...] = col_bias
    out_ref[...] = tile_ref[...] * to_column(1.0 / row_bias) * as_row(1.0 / col_bias)


def on_device(pair_rows, pair_cols, pair_weights, block_counts):
    n_row = lax.axis_size("row")
    n_col = lax.axis_size("col")
    both = ("row", "col")
    r_bins = float(TILE * n_row)
    c_bins = float(TILE * n_col)
    wider = c_bins / r_bins
    lines = TILE // LANES
    tile_type = jax.ShapeDtypeStruct((TILE, TILE), jnp.float32)
    vec_type = jax.ShapeDtypeStruct((lines, LANES), jnp.float32)

    def sent(n, k=lines):
        return jax.ShapeDtypeStruct((n, k, LANES), jnp.float32)

    def swap(x, axis):
        return lax.all_to_all(x, axis, split_axis=0, concat_axis=0, tiled=True)

    send, kept = pack(block_counts, pair_rows, pair_cols, pair_weights, n_row * n_col)
    got = swap(send, both)
    share = row_share(pair_rows, kept, n_row, n_col)
    shares = swap(share, both)
    extra = bin_extra(got)
    handed = [((r ^ 1) * n_col + r, r * n_col + r) for r in range(n_row)]
    moved = lax.ppermute(extra, both, handed)
    part = bin_main(got, extra)

    tile, first_part = pl.pallas_call(
        lambda *refs: first_kernel(c_bins, *refs), out_shape=(tile_type, sent(n_row, 2 * lines)), name="first"
    )(part, moved, shares)
    first_got = swap(first_part, "row")
    across_part = pl.pallas_call(
        lambda *refs: across_kernel(wider, *refs), out_shape=sent(n_col), name="across"
    )(tile, first_got)
    across_got = swap(across_part, "col")
    down_part = pl.pallas_call(down_kernel, out_shape=sent(n_row), name="down")(tile, across_got)
    down_got = swap(down_part, "row")
    balanced, row_bias, col_bias = pl.pallas_call(
        lambda *refs: last_kernel(r_bins, wider, *refs),
        out_shape=(tile_type, vec_type, vec_type),
        name="last",
    )(tile, first_got, across_got, down_got)
    return (balanced, row_bias.reshape(-1), col_bias.reshape(-1))


def solution(mesh):
    return jax.shard_map(
        on_device,
        mesh=mesh,
        in_specs=(
            P(("row", "col"), None),
            P(("row", "col"), None),
            P(("row", "col"), None),
            P(("row", "col")),
        ),
        out_specs=(P("row", "col"), P("row"), P("col")),
        check_vma=False,
    )
```

```python
import jax
import jax.numpy as jnp
from jax import lax
from jax.experimental import pallas as pl
from jax.experimental.pallas import tpu as pltpu
from jax.sharding import PartitionSpec as P

TILE = 512
SUB = 128
LANES = 128
SIDE = TILE // SUB
SWEEPS = 2


prior_count = 0.015625
params = pltpu.CompilerParams(vmem_limit_bytes=16 * 2**20)


def helpers(row, col_of_row, n_row, n_col):
    return [
        (row ^ 1, col_of_row),
        (row, (col_of_row + 4) % n_col),
        (row, (col_of_row + n_col - 4) % n_col),
        ((row + 2) % n_row, col_of_row),
        ((row + n_row - 2) % n_row, col_of_row),
    ]


def has_extra(row, col, n_row, n_col):
    across = (col - row + n_col) % n_col
    down = (row - col + 2 * n_row) % n_row
    near = (col == row) | (col == (row ^ 1)) | (across == 4) | (across == n_col - 4)
    return near | ((col < n_row) & ((down == 2) | (down == n_row - 2)))


def pack_kernel(n_row, n_col, counts_ref, rows_ref, cols_ref, wgt_ref, send_ref, kept_ref, stage_ref, seen_ref, sem):
    blocks, cap = rows_ref.shape
    chunks = cap // LANES
    for i in range(n_row):
        seen_ref[i] = 0

    devices = n_row * n_col
    @pl.loop(0, blocks // 8)
    def _(group):
        at = pl.ds(pl.multiple_of(group * 8, 8), 8)
        rows = rows_ref[at, :]
        cols = cols_ref[at, :]
        place = ((rows & (TILE - 1)) * TILE + (cols & (TILE - 1))).astype(jnp.float32)
        tiles = (rows[:, :1] // TILE) * n_col + cols[:, :1] // TILE
        entry = lax.broadcasted_iota(jnp.int32, (8, cap), 1)
        line = lax.broadcasted_iota(jnp.int32, (8, cap), 0)
        count = jnp.zeros((8, cap), jnp.int32)
        for r in range(8):
            count = jnp.where(line == r, counts_ref[group * 8 + r], count)
        kept = jnp.where(entry < count, wgt_ref[at, :], 0.0)
        kept_ref[at, :] = kept
        for r in range(8):
            tile = tiles[r, 0]
            tile_row = tile // n_col
            diagonal = tile_row == tile % n_col
            rank = seen_ref[tile_row]
            seen_ref[tile_row] = rank + jnp.where(diagonal, 1, 0)
            spot = jnp.where(diagonal & (rank < 2), devices + tile_row * 2 + rank, tile)
            for k in range(chunks):
                lanes = slice(LANES * k, LANES * (k + 1))
                stage_ref[spot, k : k + 1, :] = place[r : r + 1, lanes]
                stage_ref[spot, chunks + k : chunks + k + 1, :] = kept[r : r + 1, lanes]

    for tile_row in range(n_row):
        owners = [(tile_row, tile_row)] + helpers(tile_row, tile_row, n_row, n_col)
        for part, (a, b) in enumerate(owners):
            spot = devices + tile_row * 2 + part // 3
            for half in range(2):
                k = part % 3 * 2 + half
                here = 2 * chunks + half
                stage_ref[a * n_col + b, here] = stage_ref[spot, k]
                stage_ref[a * n_col + b, here + 2] = stage_ref[spot, chunks + k]

    copy = pltpu.make_async_copy(stage_ref.at[pl.ds(0, devices)], send_ref, sem)
    copy.start()
    copy.wait()


def pack(counts, rows, cols, wgt, n_row, n_col):
    blocks, cap = rows.shape
    return pl.pallas_call(
        lambda *refs: pack_kernel(n_row, n_col, *refs),
        out_shape=(
            jax.ShapeDtypeStruct((n_row * n_col, 2 * cap // LANES + 4, LANES), jnp.float32),
            jax.ShapeDtypeStruct(wgt.shape, jnp.float32),
        ),
        in_specs=[pl.BlockSpec(memory_space=pltpu.SMEM)] + [pl.BlockSpec(memory_space=pltpu.VMEM)] * 3,
        out_specs=(pl.BlockSpec(memory_space=pl.ANY), pl.BlockSpec(memory_space=pltpu.VMEM)),
        scratch_shapes=[
            pltpu.VMEM((n_row * n_col + 2 * n_row, 2 * cap // LANES + 4, LANES), jnp.float32),
            pltpu.SMEM((n_row,), jnp.int32),
            pltpu.SemaphoreType.DMA,
        ],
        compiler_params=params,
        name="pack",
    )(counts, rows, cols, wgt)


def row_share_kernel(n_col, rows_ref, kept_ref, out_ref, acc_ref):
    blocks, cap = rows_ref.shape
    acc_ref[...] = jnp.zeros_like(acc_ref)
    bins = lax.broadcasted_iota(jnp.int32, (SUB, LANES), 0)

    @pl.loop(0, blocks // 8)
    def _(group):
        at = pl.ds(pl.multiple_of(group * 8, 8), 8)
        rows = rows_ref[at, :]
        kept = kept_ref[at, :]
        local = rows & (SUB - 1)
        strips = rows[:, :1] // SUB
        for r in range(8):
            total = jnp.zeros((SUB, LANES), jnp.float32)
            for k in range(cap // LANES):
                lanes = slice(LANES * k, LANES * (k + 1))
                total += jnp.where(local[r : r + 1, lanes] == bins, kept[r : r + 1, lanes], 0.0)
            acc_ref[strips[r, 0]] += total

    for strip in range(acc_ref.shape[0]):
        column = jnp.sum(acc_ref[strip], axis=1, keepdims=True)
        sums = jnp.sum(jnp.where(same_lane(), column, 0.0), axis=0, keepdims=True)
        row, line = divmod(strip, TILE // SUB)
        for c in range(n_col):
            out_ref[row * n_col + c, line : line + 1, :] = sums


def row_share(rows, kept, n_row, n_col):
    return pl.pallas_call(
        lambda *refs: row_share_kernel(n_col, *refs),
        out_shape=jax.ShapeDtypeStruct((n_row * n_col, TILE // LANES, LANES), jnp.float32),
        scratch_shapes=[pltpu.VMEM((n_row * TILE // SUB, SUB, LANES), jnp.float32)],
        cost_estimate=pl.CostEstimate(flops=10**9, bytes_accessed=10**6, transcendentals=0),
        compiler_params=params,
        name="row_share",
    )(rows, kept)


def square_of(x, chunks):
    place = x[:chunks].astype(jnp.int32)
    wgt = x[chunks:]
    local_row = ((place >> 9) & (SUB - 1)).astype(jnp.float32)
    local_col = (place & (SUB - 1)).astype(jnp.float32)
    high = wgt.astype(jnp.bfloat16).astype(jnp.float32)
    rest = wgt - high
    bins = lax.broadcasted_iota(jnp.int32, (SUB, LANES), 0).astype(jnp.bfloat16)
    one = jnp.ones((SUB, LANES), jnp.bfloat16)
    zero = jnp.zeros((SUB, LANES), jnp.bfloat16)

    def spread(v, k):
        return jnp.broadcast_to(v[k : k + 1], (SUB, LANES)).astype(jnp.bfloat16)

    row_hot, high_hot, rest_hot = [], [], []
    for k in range(chunks):
        row_hot.append(jnp.where(spread(local_row, k) == bins, one, zero))
        hit = spread(local_col, k) == bins
        high_hot.append(jnp.where(hit, spread(high, k), zero))
        rest_hot.append(jnp.where(hit, spread(rest, k), zero))
    row_hot = jnp.concatenate(row_hot, axis=1)
    col_hot = jnp.concatenate(
        [jnp.concatenate(high_hot, axis=1), jnp.concatenate(rest_hot, axis=1)], axis=0
    )
    both = lax.dot_general(
        row_hot, col_hot, (((1,), (1,)), ((), ())), preferred_element_type=jnp.float32
    )
    return both[:, :SUB] + both[:, SUB:]


def add_blocks(got_ref, first, lines, acc_ref, unroll):
    sources = got_ref.shape[0]

    @pl.loop(0, sources // unroll)
    def _(step):
        for u in range(unroll):
            x = got_ref[step * unroll + u, first : first + lines, :]
            head = x[0, 0].astype(jnp.int32)
            square = (head >> 16) * SIDE + ((head >> 7) & (SIDE - 1))
            acc_ref[square] += square_of(x, lines // 2)


def write_tile(acc_ref, out_ref):
    for i in range(SIDE):
        for j in range(SIDE):
            out_ref[SUB * i : SUB * (i + 1), SUB * j : SUB * (j + 1)] = acc_ref[i * SIDE + j]


def extra_kernel(n_row, n_col, got_ref, out_ref, acc_ref):
    step = pl.program_id(0)

    @pl.when(has_extra(lax.axis_index("row"), lax.axis_index("col"), n_row, n_col))
    def _():
        @pl.when(step == 0)
        def _():
            acc_ref[...] = jnp.zeros_like(acc_ref)

        add_blocks(got_ref, got_ref.shape[1] - 4, 4, acc_ref, bin_unroll)

        @pl.when(step == pl.num_programs(0) - 1)
        def _():
            write_tile(acc_ref, out_ref)


def main_kernel(got_ref, out_ref, acc_ref):
    step = pl.program_id(0)

    @pl.when(step == 0)
    def _():
        acc_ref[...] = jnp.zeros_like(acc_ref)

    add_blocks(got_ref, 0, got_ref.shape[1] - 4, acc_ref, bin_unroll)

    @pl.when(step == pl.num_programs(0) - 1)
    def _():
        write_tile(acc_ref, out_ref)


bin_steps = 4
bin_unroll = 8


def bin_blocks(kernel, got, name, flops):
    sources = got.shape[0]
    return pl.pallas_call(
        kernel,
        grid=(bin_steps,),
        out_shape=jax.ShapeDtypeStruct((TILE, TILE), jnp.float32),
        in_specs=[pl.BlockSpec((sources // bin_steps,) + got.shape[1:], lambda i: (i, 0, 0))],
        out_specs=pl.BlockSpec((TILE, TILE), lambda i: (0, 0)),
        scratch_shapes=[pltpu.VMEM((SIDE * SIDE, SUB, SUB), jnp.float32)],
        cost_estimate=pl.CostEstimate(flops=flops, bytes_accessed=2 * 10**6, transcendentals=0),
        compiler_params=params,
        name=name,
    )(got)


def to_lanes(column):
    return jnp.concatenate(
        [
            jnp.sum(jnp.where(same_lane(), column[LANES * k : LANES * (k + 1)], 0.0), axis=0, keepdims=True)
            for k in range(TILE // LANES)
        ],
        axis=0,
    )


def same_lane():
    down = lax.broadcasted_iota(jnp.int32, (LANES, LANES), 0)
    across = lax.broadcasted_iota(jnp.int32, (LANES, LANES), 1)
    return down == across


def to_column(vec):
    return jnp.concatenate(
        [
            jnp.sum(jnp.where(same_lane(), vec[k : k + 1], 0.0), axis=1, keepdims=True)
            for k in range(vec.shape[0])
        ],
        axis=0,
    )


def as_row(vec):
    return jnp.concatenate([vec[k : k + 1] for k in range(vec.shape[0])], axis=1)


def from_row(row):
    return jnp.concatenate(
        [row[:, LANES * k : LANES * (k + 1)] for k in range(TILE // LANES)], axis=0
    )


def first_kernel(c_bins, part_ref, got_ref, *refs):
    handed_refs, (tile_ref, out_ref, held_ref, sems) = refs[:-4], refs[-4:]
    tile_ref[...] = part_ref[...] + prior_count

    @pl.when(lax.axis_index("row") == lax.axis_index("col"))
    def _():
        copies = [
            pltpu.make_async_copy(ref, held_ref.at[i], sems.at[i]) for i, ref in enumerate(handed_refs)
        ]
        for copy in copies:
            copy.start()
        for copy in copies:
            copy.wait()
        total = tile_ref[...]
        for i in range(len(copies)):
            total += held_ref[i]
        tile_ref[...] = total

    row_sums = jnp.sum(got_ref[...], axis=0) + c_bins * prior_count
    total = jnp.sum(row_sums, axis=1, keepdims=True)
    sums = from_row(jnp.sum(tile_ref[...] * to_column(1.0 / row_sums), axis=0, keepdims=True))
    send = jnp.concatenate([sums, jnp.broadcast_to(total, sums.shape)], axis=0)
    for d in range(out_ref.shape[0]):
        out_ref[d] = send


def across_kernel(wider, tile_ref, got_ref, out_ref):
    vec = jnp.sum(got_ref[:, : TILE // LANES, :], axis=0) * wider
    sums = to_lanes(jnp.sum(tile_ref[...] * as_row(1.0 / vec), axis=1, keepdims=True))
    for d in range(out_ref.shape[0]):
        out_ref[d] = sums


def down_kernel(tile_ref, got_ref, out_ref):
    vec = jnp.sum(got_ref[...], axis=0)
    sums = from_row(jnp.sum(tile_ref[...] * to_column(1.0 / vec), axis=0, keepdims=True))
    for d in range(out_ref.shape[0]):
        out_ref[d] = sums


def last_kernel(r_bins, wider, tile_ref, first_ref, across_ref, down_ref, out_ref, row_ref, col_ref):
    total = jnp.sum(first_ref[:, TILE // LANES :, 0:1], axis=(0, 1), keepdims=True)[0]
    row_mean = total / r_bins
    row_bias = jnp.sum(across_ref[...], axis=0) / row_mean
    col_bias = jnp.sum(down_ref[...], axis=0) * wider
    row_ref[...] = row_bias
    col_ref[...] = col_bias
    out_ref[...] = tile_ref[...] * to_column(1.0 / row_bias) * as_row(1.0 / col_bias)


def on_device(pair_rows, pair_cols, pair_weights, block_counts):
    n_row = lax.axis_size("row")
    n_col = lax.axis_size("col")
    both = ("row", "col")
    r_bins = float(TILE * n_row)
    c_bins = float(TILE * n_col)
    wider = c_bins / r_bins
    lines = TILE // LANES
    tile_type = jax.ShapeDtypeStruct((TILE, TILE), jnp.float32)
    vec_type = jax.ShapeDtypeStruct((lines, LANES), jnp.float32)

    def sent(n, k=lines):
        return jax.ShapeDtypeStruct((n, k, LANES), jnp.float32)

    def swap(x, axis):
        return lax.all_to_all(x, axis, split_axis=0, concat_axis=0, tiled=True)

    send, kept = pack(block_counts, pair_rows, pair_cols, pair_weights, n_row, n_col)
    got = swap(send, both)
    share = row_share(pair_rows, kept, n_row, n_col)
    got, share = lax.optimization_barrier((got, share))
    shares = swap(share, both)
    extra = bin_blocks(lambda *refs: extra_kernel(n_row, n_col, *refs), got, "bin_extra", 3 * 10**9)
    pairs = [[] for _ in range(5)]
    for r in range(n_row):
        for i, (a, b) in enumerate(helpers(r, r, n_row, n_col)):
            pairs[i].append((a * n_col + b, r * n_col + r))
    handed = [extra] + [lax.ppermute(extra, both, p) for p in pairs]
    part = bin_blocks(main_kernel, got, "bin_main", 10**10)

    in_vmem = pl.BlockSpec(memory_space=pltpu.VMEM)
    tile, first_part = pl.pallas_call(
        lambda *refs: first_kernel(c_bins, *refs),
        out_shape=(tile_type, sent(n_row, 2 * lines)),
        in_specs=[in_vmem] * 2 + [pl.BlockSpec(memory_space=pl.ANY)] * len(handed),
        out_specs=(in_vmem, in_vmem),
        scratch_shapes=[
            pltpu.VMEM((len(handed), TILE, TILE), jnp.float32),
            pltpu.SemaphoreType.DMA((len(handed),)),
        ],
        compiler_params=params,
        name="first",
    )(part, shares, *handed)
    first_got = swap(first_part, "row")
    across_part = pl.pallas_call(
        lambda *refs: across_kernel(wider, *refs), out_shape=sent(n_col), name="across", compiler_params=params
    )(tile, first_got)
    across_got = swap(across_part, "col")
    down_part = pl.pallas_call(down_kernel, out_shape=sent(n_row), name="down", compiler_params=params)(tile, across_got)
    down_got = swap(down_part, "row")
    balanced, row_bias, col_bias = pl.pallas_call(
        lambda *refs: last_kernel(r_bins, wider, *refs),
        out_shape=(tile_type, vec_type, vec_type),
        compiler_params=params,
        name="last",
    )(tile, first_got, across_got, down_got)
    return (balanced, row_bias.reshape(-1), col_bias.reshape(-1))


def solution(mesh):
    return jax.shard_map(
        on_device,
        mesh=mesh,
        in_specs=(
            P(("row", "col"), None),
            P(("row", "col"), None),
            P(("row", "col"), None),
            P(("row", "col")),
        ),
        out_specs=(P("row", "col"), P("row"), P("col")),
        check_vma=False,
    )
```

```python
import jax
import jax.numpy as jnp
from jax import lax
from jax.experimental import pallas as pl
from jax.experimental.pallas import tpu as pltpu
from jax.sharding import PartitionSpec as P

TILE = 512
SUB = 128
LANES = 128
SIDE = TILE // SUB
SWEEPS = 2


prior_count = 0.015625
params = pltpu.CompilerParams(vmem_limit_bytes=16 * 2**20)


def helpers(row, col_of_row, n_row, n_col):
    return [
        (row ^ 1, col_of_row),
        (row, (col_of_row + 4) % n_col),
        (row, (col_of_row + n_col - 4) % n_col),
        ((row + 2) % n_row, col_of_row),
        ((row + n_row - 2) % n_row, col_of_row),
    ]


def has_extra(row, col, n_row, n_col):
    across = (col - row + n_col) % n_col
    down = (row - col + 2 * n_row) % n_row
    near = (col == row) | (col == (row ^ 1)) | (across == 4) | (across == n_col - 4)
    return near | ((col < n_row) & ((down == 2) | (down == n_row - 2)))


def pack_kernel(
    n_row, n_col, counts_hbm, rows_hbm, cols_hbm, wgt_hbm,
    send_ref, kept_ref, stage_ref, rows_ref, cols_ref, wgt_ref, counts_ref, seen_ref, sems, sem,
):
    blocks, cap = rows_ref.shape
    chunks = cap // LANES
    col_bits = n_col.bit_length() - 1
    parts = sems.shape[0]
    size = blocks // parts
    pltpu.make_async_copy(counts_hbm, counts_ref, sem).start()
    copies = []
    for i in range(parts):
        at = pl.ds(size * i, size)
        pairs = ((rows_hbm, rows_ref), (cols_hbm, cols_ref), (wgt_hbm, wgt_ref))
        copies.append(
            [pltpu.make_async_copy(a.at[at], b.at[at], sems.at[i, k]) for k, (a, b) in enumerate(pairs)]
        )
        for copy in copies[-1]:
            copy.start()
    for i in range(n_row):
        seen_ref[i] = 0
    pltpu.make_async_copy(counts_hbm, counts_ref, sem).wait()

    devices = n_row * n_col

    def pack_group(group):
        at = pl.ds(pl.multiple_of(group * 8, 8), 8)
        rows = rows_ref[at, :]
        cols = cols_ref[at, :]
        place = ((rows & (TILE - 1)) * TILE + (cols & (TILE - 1))).astype(jnp.float32)
        tiles = ((rows[:, :1] >> 9) << col_bits) + (cols[:, :1] >> 9)
        entry = lax.broadcasted_iota(jnp.int32, (8, cap), 1)
        line = lax.broadcasted_iota(jnp.int32, (8, cap), 0)
        count = jnp.zeros((8, cap), jnp.int32)
        for r in range(8):
            count = jnp.where(line == r, counts_ref[group * 8 + r], count)
        kept = jnp.where(entry < count, wgt_ref[at, :], 0.0)
        kept_ref[at, :] = kept
        for r in range(8):
            tile = tiles[r, 0]
            tile_row = tile >> col_bits
            diagonal = tile == tile_row * (n_col + 1)
            rank = seen_ref[tile_row]
            seen_ref[tile_row] = rank + jnp.where(diagonal, 1, 0)
            spot = jnp.where(diagonal & (rank < 2), devices + tile_row * 2 + rank, tile)
            for k in range(chunks):
                lanes = slice(LANES * k, LANES * (k + 1))
                stage_ref[spot, k : k + 1, :] = place[r : r + 1, lanes]
                stage_ref[spot, chunks + k : chunks + k + 1, :] = kept[r : r + 1, lanes]

    for i in range(parts):
        for copy in copies[i]:
            copy.wait()

        @pl.loop(i * size // 8, (i + 1) * size // 8)
        def _(group):
            pack_group(group)

    for tile_row in range(n_row):
        owners = [(tile_row, tile_row)] + helpers(tile_row, tile_row, n_row, n_col)
        for part, (a, b) in enumerate(owners):
            spot = devices + tile_row * 2 + part // 3
            for half in range(2):
                k = part % 3 * 2 + half
                here = 2 * chunks + half
                stage_ref[a * n_col + b, here] = stage_ref[spot, k]
                stage_ref[a * n_col + b, here + 2] = stage_ref[spot, chunks + k]

    copy = pltpu.make_async_copy(stage_ref.at[pl.ds(0, devices)], send_ref, sem)
    copy.start()
    copy.wait()


def pack(counts, rows, cols, wgt, n_row, n_col):
    blocks, cap = rows.shape
    return pl.pallas_call(
        lambda *refs: pack_kernel(n_row, n_col, *refs),
        out_shape=(
            jax.ShapeDtypeStruct((n_row * n_col, 2 * cap // LANES + 4, LANES), jnp.float32),
            jax.ShapeDtypeStruct(wgt.shape, jnp.float32),
        ),
        in_specs=[pl.BlockSpec(memory_space=pltpu.HBM)] * 4,
        out_specs=(pl.BlockSpec(memory_space=pltpu.HBM), pl.BlockSpec(memory_space=pltpu.VMEM)),
        scratch_shapes=[
            pltpu.VMEM((n_row * n_col + 2 * n_row, 2 * cap // LANES + 4, LANES), jnp.float32),
            pltpu.VMEM(rows.shape, jnp.int32),
            pltpu.VMEM(cols.shape, jnp.int32),
            pltpu.VMEM(wgt.shape, jnp.float32),
            pltpu.SMEM(counts.shape, jnp.int32),
            pltpu.SMEM((n_row,), jnp.int32),
            pltpu.SemaphoreType.DMA((3, 3)),
            pltpu.SemaphoreType.DMA,
        ],
        compiler_params=pltpu.CompilerParams(vmem_limit_bytes=60 * 2**20),
        name="pack",
    )(counts, rows, cols, wgt)


def row_share_kernel(n_col, rows_ref, kept_ref, out_ref, acc_ref):
    blocks, cap = rows_ref.shape
    acc_ref[...] = jnp.zeros_like(acc_ref)
    bins = lax.broadcasted_iota(jnp.int32, (SUB, LANES), 0)

    @pl.loop(0, blocks // 8)
    def _(group):
        at = pl.ds(pl.multiple_of(group * 8, 8), 8)
        rows = rows_ref[at, :]
        kept = kept_ref[at, :]
        local = rows & (SUB - 1)
        strips = rows[:, :1] // SUB
        for r in range(8):
            total = jnp.zeros((SUB, LANES), jnp.float32)
            for k in range(cap // LANES):
                lanes = slice(LANES * k, LANES * (k + 1))
                total += jnp.where(local[r : r + 1, lanes] == bins, kept[r : r + 1, lanes], 0.0)
            acc_ref[strips[r, 0]] += total

    for strip in range(acc_ref.shape[0]):
        column = jnp.sum(acc_ref[strip], axis=1, keepdims=True)
        sums = jnp.sum(jnp.where(same_lane(), column, 0.0), axis=0, keepdims=True)
        row, line = divmod(strip, TILE // SUB)
        for c in range(n_col):
            out_ref[row * n_col + c, line : line + 1, :] = sums


def row_share(rows, kept, n_row, n_col):
    return pl.pallas_call(
        lambda *refs: row_share_kernel(n_col, *refs),
        out_shape=jax.ShapeDtypeStruct((n_row * n_col, TILE // LANES, LANES), jnp.float32),
        scratch_shapes=[pltpu.VMEM((n_row * TILE // SUB, SUB, LANES), jnp.float32)],
        cost_estimate=pl.CostEstimate(flops=10**9, bytes_accessed=10**6, transcendentals=0),
        compiler_params=params,
        name="row_share",
    )(rows, kept)


def square_of(x, chunks):
    place = x[:chunks].astype(jnp.int32)
    wgt = x[chunks:]
    local_row = ((place >> 9) & (SUB - 1)).astype(jnp.float32)
    local_col = (place & (SUB - 1)).astype(jnp.float32)
    high = wgt.astype(jnp.bfloat16).astype(jnp.float32)
    rest = wgt - high
    bins = lax.broadcasted_iota(jnp.int32, (SUB, LANES), 0).astype(jnp.bfloat16)
    one = jnp.ones((SUB, LANES), jnp.bfloat16)
    zero = jnp.zeros((SUB, LANES), jnp.bfloat16)

    def spread(v, k):
        return jnp.broadcast_to(v[k : k + 1], (SUB, LANES)).astype(jnp.bfloat16)

    row_hot, high_hot, rest_hot = [], [], []
    for k in range(chunks):
        row_hot.append(jnp.where(spread(local_row, k) == bins, one, zero))
        hit = spread(local_col, k) == bins
        high_hot.append(jnp.where(hit, spread(high, k), zero))
        rest_hot.append(jnp.where(hit, spread(rest, k), zero))
    row_hot = jnp.concatenate(row_hot, axis=1)
    col_hot = jnp.concatenate(
        [jnp.concatenate(high_hot, axis=1), jnp.concatenate(rest_hot, axis=1)], axis=0
    )
    both = lax.dot_general(
        row_hot, col_hot, (((1,), (1,)), ((), ())), preferred_element_type=jnp.float32
    )
    return both[:, :SUB] + both[:, SUB:]


def add_blocks(got_ref, first, lines, acc_ref, unroll):
    sources = got_ref.shape[0]

    @pl.loop(0, sources // unroll)
    def _(step):
        for u in range(unroll):
            x = got_ref[step * unroll + u, first : first + lines, :]
            head = x[0, 0].astype(jnp.int32)
            square = (head >> 16) * SIDE + ((head >> 7) & (SIDE - 1))
            acc_ref[square] += square_of(x, lines // 2)


def write_tile(acc_ref, out_ref):
    for i in range(SIDE):
        for j in range(SIDE):
            out_ref[SUB * i : SUB * (i + 1), SUB * j : SUB * (j + 1)] = acc_ref[i * SIDE + j]


def extra_kernel(n_row, n_col, got_ref, out_ref, acc_ref):
    step = pl.program_id(0)

    @pl.when(has_extra(lax.axis_index("row"), lax.axis_index("col"), n_row, n_col))
    def _():
        @pl.when(step == 0)
        def _():
            acc_ref[...] = jnp.zeros_like(acc_ref)

        add_blocks(got_ref, got_ref.shape[1] - 4, 4, acc_ref, bin_unroll)

        @pl.when(step == pl.num_programs(0) - 1)
        def _():
            write_tile(acc_ref, out_ref)


def main_kernel(got_ref, out_ref, acc_ref):
    step = pl.program_id(0)

    @pl.when(step == 0)
    def _():
        acc_ref[...] = jnp.full_like(acc_ref, prior_count)

    add_blocks(got_ref, 0, got_ref.shape[1] - 4, acc_ref, bin_unroll)

    @pl.when(step == pl.num_programs(0) - 1)
    def _():
        write_tile(acc_ref, out_ref)


bin_steps = 4
bin_unroll = 8


def bin_blocks(kernel, got, name, flops):
    sources = got.shape[0]
    return pl.pallas_call(
        kernel,
        grid=(bin_steps,),
        out_shape=jax.ShapeDtypeStruct((TILE, TILE), jnp.float32),
        in_specs=[pl.BlockSpec((sources // bin_steps,) + got.shape[1:], lambda i: (i, 0, 0))],
        out_specs=pl.BlockSpec((TILE, TILE), lambda i: (0, 0)),
        scratch_shapes=[pltpu.VMEM((SIDE * SIDE, SUB, SUB), jnp.float32)],
        cost_estimate=pl.CostEstimate(flops=flops, bytes_accessed=2 * 10**6, transcendentals=0),
        compiler_params=params,
        name=name,
    )(got)


def to_lanes(column):
    return jnp.concatenate(
        [
            jnp.sum(jnp.where(same_lane(), column[LANES * k : LANES * (k + 1)], 0.0), axis=0, keepdims=True)
            for k in range(TILE // LANES)
        ],
        axis=0,
    )


def same_lane():
    down = lax.broadcasted_iota(jnp.int32, (LANES, LANES), 0)
    across = lax.broadcasted_iota(jnp.int32, (LANES, LANES), 1)
    return down == across


def to_column(vec):
    return jnp.concatenate(
        [
            jnp.sum(jnp.where(same_lane(), vec[k : k + 1], 0.0), axis=1, keepdims=True)
            for k in range(vec.shape[0])
        ],
        axis=0,
    )


def as_row(vec):
    return jnp.concatenate([vec[k : k + 1] for k in range(vec.shape[0])], axis=1)


def from_row(row):
    return jnp.concatenate(
        [row[:, LANES * k : LANES * (k + 1)] for k in range(TILE // LANES)], axis=0
    )


def first_kernel(c_bins, part_ref, got_ref, extra_ref, *refs):
    handed_refs, (tile_ref, out_ref, held_ref, sems) = refs[:-4], refs[-4:]

    @pl.when(lax.axis_index("row") == lax.axis_index("col"))
    def _():
        copies = [
            pltpu.make_async_copy(ref, held_ref.at[i], sems.at[i]) for i, ref in enumerate(handed_refs)
        ]
        for copy in copies:
            copy.start()

        def add(*terms):
            @pl.loop(0, TILE // 32)
            def _(strip):
                at = pl.ds(pl.multiple_of(strip * 32, 32), 32)
                total = terms[0][at, :]
                for term in terms[1:]:
                    total += term[at, :]
                tile_ref[at, :] = total

        copies[0].wait()
        copies[1].wait()
        add(part_ref, extra_ref, held_ref.at[0], held_ref.at[1])
        for copy in copies[2:]:
            copy.wait()
        add(tile_ref, *(held_ref.at[i] for i in range(2, len(copies))))

    row_sums = jnp.sum(got_ref[...], axis=0) + c_bins * prior_count
    total = jnp.sum(row_sums, axis=1, keepdims=True)
    sums = from_row(jnp.sum(tile_ref[...] * to_column(1.0 / row_sums), axis=0, keepdims=True))
    send = jnp.concatenate([sums, jnp.broadcast_to(total, sums.shape)], axis=0)
    for d in range(out_ref.shape[0]):
        out_ref[d] = send


def across_kernel(wider, tile_ref, got_ref, out_ref):
    vec = jnp.sum(got_ref[:, : TILE // LANES, :], axis=0) * wider
    sums = to_lanes(jnp.sum(tile_ref[...] * as_row(1.0 / vec), axis=1, keepdims=True))
    for d in range(out_ref.shape[0]):
        out_ref[d] = sums


def down_kernel(tile_ref, got_ref, out_ref):
    vec = jnp.sum(got_ref[...], axis=0)
    sums = from_row(jnp.sum(tile_ref[...] * to_column(1.0 / vec), axis=0, keepdims=True))
    for d in range(out_ref.shape[0]):
        out_ref[d] = sums


def last_kernel(r_bins, wider, tile_ref, first_ref, across_ref, down_ref, out_ref, row_ref, col_ref):
    total = jnp.sum(first_ref[:, TILE // LANES :, 0:1], axis=(0, 1), keepdims=True)[0]
    row_mean = total / r_bins
    row_bias = jnp.sum(across_ref[...], axis=0) / row_mean
    col_bias = jnp.sum(down_ref[...], axis=0) * wider
    row_ref[...] = row_bias
    col_ref[...] = col_bias
    out_ref[...] = tile_ref[...] * to_column(1.0 / row_bias) * as_row(1.0 / col_bias)


def on_device(pair_rows, pair_cols, pair_weights, block_counts):
    n_row = lax.axis_size("row")
    n_col = lax.axis_size("col")
    both = ("row", "col")
    r_bins = float(TILE * n_row)
    c_bins = float(TILE * n_col)
    wider = c_bins / r_bins
    lines = TILE // LANES
    tile_type = jax.ShapeDtypeStruct((TILE, TILE), jnp.float32)
    vec_type = jax.ShapeDtypeStruct((lines, LANES), jnp.float32)

    def sent(n, k=lines):
        return jax.ShapeDtypeStruct((n, k, LANES), jnp.float32)

    def swap(x, axis):
        return lax.all_to_all(x, axis, split_axis=0, concat_axis=0, tiled=True)

    send, kept = pack(block_counts, pair_rows, pair_cols, pair_weights, n_row, n_col)
    got = swap(send, both)
    share = row_share(pair_rows, kept, n_row, n_col)
    got, share = lax.optimization_barrier((got, share))
    shares = swap(share, both)
    extra = bin_blocks(lambda *refs: extra_kernel(n_row, n_col, *refs), got, "bin_extra", 3 * 10**9)
    handed = []
    for i in range(5):
        trade = list(range(n_row * n_col))
        for r in range(n_row):
            a, b = helpers(r, r, n_row, n_col)[i]
            trade[a * n_col + b], trade[r * n_col + r] = r * n_col + r, a * n_col + b
        handed.append(lax.ppermute(extra, both, list(enumerate(trade))))
    part = bin_blocks(main_kernel, got, "bin_main", 10**10)

    in_vmem = pl.BlockSpec(memory_space=pltpu.VMEM)
    tile, first_part = pl.pallas_call(
        lambda *refs: first_kernel(c_bins, *refs),
        out_shape=(tile_type, sent(n_row, 2 * lines)),
        in_specs=[in_vmem] * 3 + [pl.BlockSpec(memory_space=pl.ANY)] * len(handed),
        out_specs=(in_vmem, in_vmem),
        scratch_shapes=[
            pltpu.VMEM((len(handed), TILE, TILE), jnp.float32),
            pltpu.SemaphoreType.DMA((len(handed),)),
        ],
        input_output_aliases={0: 0},
        compiler_params=params,
        name="first",
    )(part, shares, extra, *handed)
    first_got = swap(first_part, "row")
    across_part = pl.pallas_call(
        lambda *refs: across_kernel(wider, *refs), out_shape=sent(n_col), name="across", compiler_params=params
    )(tile, first_got)
    across_got = swap(across_part, "col")
    down_part = pl.pallas_call(down_kernel, out_shape=sent(n_row), name="down", compiler_params=params)(tile, across_got)
    down_got = swap(down_part, "row")
    balanced, row_bias, col_bias = pl.pallas_call(
        lambda *refs: last_kernel(r_bins, wider, *refs),
        out_shape=(tile_type, vec_type, vec_type),
        compiler_params=params,
        name="last",
    )(tile, first_got, across_got, down_got)
    return (balanced, row_bias.reshape(-1), col_bias.reshape(-1))


def solution(mesh):
    return jax.shard_map(
        on_device,
        mesh=mesh,
        in_specs=(
            P(("row", "col"), None),
            P(("row", "col"), None),
            P(("row", "col"), None),
            P(("row", "col")),
        ),
        out_specs=(P("row", "col"), P("row"), P("col")),
        check_vma=False,
    )
```
